128 devices in a mesh: seq: 8 (over y_lo, x), dp: 16 (over y_hi, z, core).
Axes of the slice: x: 4, y: 4 (y_hi: 2, y_lo: 2; y = y_hi * 2 + y_lo), z: 4, core: 2. Of those that a mesh axis runs over, the one named last changes fastest.
Arguments:
- frames_in: bfloat16 [16, 8, 16, 320, 128], P('dp', 'seq'), may hold values from -6 to 6
- spatial_kernel: bfloat16 [9, 320, 320], P(None, 'seq'), may hold values from -0.109375 to 0.109375
- temporal_kernel: bfloat16 [3, 320, 320], P(None, 'seq'), may hold values from -0.1875 to 0.1875
- out_cotangent: bfloat16 [16, 8, 16, 320, 128], P('dp', 'seq'), may hold values from -6 to 6
Outputs:
- block_out: bfloat16 [16, 8, 16, 320, 128], P('dp', 'seq')
- input_grad: bfloat16 [16, 8, 16, 320, 128], P('dp', 'seq')
- spatial_grad: float32 [9, 320, 320], P(None, 'seq')
- temporal_grad: float32 [3, 320, 320], P(None, 'seq')
The draws below stay inside these ranges and needn't reach their ends.
All inputs are finite; a program needn't handle non-finite values.
Results may differ from the reference program's by a relative error of at most 0.0055.
Values may be sent and summed in bfloat16 or wider, within the bound.
A program may use at most 128 MiB of HBM per device.

```python
import math
import jax
import jax.numpy as jnp
from jax import lax

C = 320
WIDTH = 128
FRAMES = 8
HEIGHT = 16
CLIPS = 16


def raised(result, rng, source, target, blocks, factor):
    owner, partner = [(jnp.arange(result.shape[axis_at]) // (result.shape[axis_at] // blocks)).reshape([-1 if axis == axis_at else 1 for axis in range(result.ndim)]) for axis_at in (source, target)]
    chosen = jax.random.permutation(rng, blocks)[partner]
    strong = (owner == chosen) | (owner == (partner + blocks // 2) % blocks)
    return jnp.where(strong, factor * result, result)


def block_levels(stream_key, dims, cuts, smallest, top_value):
    factor_of = 1.0
    for position, parts in cuts:
        heights = jax.random.uniform(jax.random.fold_in(jax.random.fold_in(stream_key, 6), position), (parts,), jnp.float32, smallest / len(cuts), top_value / len(cuts))
        factor_of = factor_of * jnp.repeat(jnp.exp(heights), dims[position] // parts).reshape((-1,) + (1,) * (len(dims) - 1 - position))
    return factor_of


def bell_draw(rng, shape, deviation, limit, cuts=(), dtype=jnp.bfloat16):
    array = deviation * jax.random.normal(rng, shape, jnp.float32)
    if cuts:
        array = array * block_levels(rng, shape, cuts, -0.22, 0.18)
    return jnp.clip(array, -limit, limit).astype(dtype)


def bell_draw_with(rng, extent, scale, reach, shards, heavy, held_as=jnp.bfloat16):
    drawn = scale * jax.random.normal(rng, extent, jnp.float32)
    if shards:
        drawn = drawn * block_levels(rng, extent, shards, -0.22, 0.18)
    return jnp.clip(raised(drawn, jax.random.fold_in(rng, 3), *heavy), -reach, reach).astype(held_as)


def setup_inputs(seed: int = 0) -> dict:
    keys = jax.random.split(jax.random.key(seed), 5)
    return {
        "frames_in": bell_draw(keys[0], (CLIPS, FRAMES, HEIGHT, C, WIDTH), 1.0, 6.0, ((0, 16), (1, 8))),
        "spatial_kernel": bell_draw(keys[1], (9, C, C), (9 * C) ** -0.5, 0.109375, ((1, 8),)),
        "temporal_kernel": bell_draw(keys[2], (3, C, C), (3 * C) ** -0.5, 0.1875, ((1, 8),)),
        "out_cotangent": bell_draw_with(keys[3], (CLIPS, FRAMES, HEIGHT, C, WIDTH), 1.0, 6.0, ((0, 16), (1, 8)), (1, 3, 8, 2.0)),
    }


def pad_frames(values):
    return jnp.pad(values, ((0, 0), (1, 1), (0, 0), (0, 0), (0, 0)))

def pad_pixels(values):
    return jnp.pad(values, ((0, 0), (0, 0), (1, 1), (0, 0), (1, 1)))

def spatial_forward(frames, kernel):
    row_count = frames.shape[2]
    col_count = frames.shape[4]
    padded = pad_pixels(frames).astype(jnp.float32)
    kernel_wide = kernel.astype(jnp.float32)
    running = jnp.zeros(frames.shape[:3] + (kernel.shape[1], col_count), jnp.float32)
    for offset_row in range(3):
        for offset_col in range(3):
            window = padded[:, :, offset_row:offset_row + row_count, :, offset_col:offset_col + col_count]
            running = running + jnp.einsum('oc,bfhcw->bfhow', kernel_wide[3 * offset_row + offset_col], window)
    return running

def spatial_backward(pre_grad, kernel):
    row_count = pre_grad.shape[2]
    col_count = pre_grad.shape[4]
    padded = pad_pixels(pre_grad).astype(jnp.float32)
    kernel_wide = kernel.astype(jnp.float32)
    running = jnp.zeros(pre_grad.shape[:3] + (kernel.shape[2], col_count), jnp.float32)
    for offset_row in range(3):
        for offset_col in range(3):
            window = padded[:, :, 2 - offset_row:2 - offset_row + row_count, :, 2 - offset_col:2 - offset_col + col_count]
            running = running + jnp.einsum('oc,bfhow->bfhcw', kernel_wide[3 * offset_row + offset_col], window)
    return running

def spatial_weight_grad(frames, pre_grad):
    row_count = frames.shape[2]
    col_count = frames.shape[4]
    padded = pad_pixels(frames).astype(jnp.float32)
    grad_wide = pre_grad.astype(jnp.float32)
    pieces = []
    for offset_row in range(3):
        for offset_col in range(3):
            window = padded[:, :, offset_row:offset_row + row_count, :, offset_col:offset_col + col_count]
            pieces.append(jnp.einsum('bfhow,bfhcw->oc', grad_wide, window))
    return jnp.stack(pieces)

def temporal_forward(padded_act, kernel):
    frame_count = padded_act.shape[1] - 2
    padded = padded_act.astype(jnp.float32)
    kernel_wide = kernel.astype(jnp.float32)
    running = jnp.zeros(padded.shape[:1] + (frame_count,) + padded.shape[2:3] + (kernel.shape[1], padded.shape[4]), jnp.float32)
    for offset in range(3):
        running = running + jnp.einsum('oc,bfhcw->bfhow', kernel_wide[offset], padded[:, offset:offset + frame_count])
    return running

def temporal_backward(padded_cot, kernel):
    frame_count = padded_cot.shape[1] - 2
    padded = padded_cot.astype(jnp.float32)
    kernel_wide = kernel.astype(jnp.float32)
    running = jnp.zeros(padded.shape[:1] + (frame_count,) + padded.shape[2:3] + (kernel.shape[2], padded.shape[4]), jnp.float32)
    for offset in range(3):
        running = running + jnp.einsum('oc,bfhow->bfhcw', kernel_wide[offset], padded[:, 2 - offset:2 - offset + frame_count])
    return running

def temporal_weight_grad(cotangent, padded_act):
    frame_count = cotangent.shape[1]
    cot_wide = cotangent.astype(jnp.float32)
    padded = padded_act.astype(jnp.float32)
    pieces = []
    for offset in range(3):
        pieces.append(jnp.einsum('bfhow,bfhcw->oc', cot_wide, padded[:, offset:offset + frame_count]))
    return jnp.stack(pieces)

def clip_pass(frames, cotangent, spatial_kernel, temporal_kernel):
    frames = frames[None]
    cotangent = cotangent[None]
    pre_act = lax.optimization_barrier(spatial_forward(frames, spatial_kernel).astype(jnp.bfloat16))
    pre_wide = pre_act.astype(jnp.float32)
    activated = jax.nn.silu(pre_wide).astype(jnp.bfloat16)
    padded_act = pad_frames(activated)
    temporal = lax.optimization_barrier(temporal_forward(padded_act, temporal_kernel).astype(jnp.bfloat16))
    block_out = (frames.astype(jnp.float32) + temporal.astype(jnp.float32)).astype(jnp.bfloat16)
    act_grad = lax.optimization_barrier(temporal_backward(pad_frames(cotangent), temporal_kernel).astype(jnp.bfloat16))
    temporal_part = temporal_weight_grad(cotangent, padded_act)
    sigmoid_value = jax.nn.sigmoid(pre_wide)
    pre_grad = (act_grad.astype(jnp.float32) * sigmoid_value * (1.0 + pre_wide * (1.0 - sigmoid_value))).astype(jnp.bfloat16)
    spatial_part = spatial_weight_grad(frames, pre_grad)
    input_grad = (cotangent.astype(jnp.float32) + spatial_backward(pre_grad, spatial_kernel)).astype(jnp.bfloat16)
    return (block_out[0], input_grad[0], spatial_part, temporal_part)

def reference(frames_in, spatial_kernel, temporal_kernel, out_cotangent):

    def one_clip(clip_pair):
        return clip_pass(clip_pair[0], clip_pair[1], spatial_kernel, temporal_kernel)
    results = lax.map(one_clip, (frames_in, out_cotangent))
    grad_scale = 1.0 / math.sqrt(CLIPS * FRAMES * HEIGHT * WIDTH)
    spatial_grad = lax.optimization_barrier(jnp.sum(results[2], axis=0)) * grad_scale
    temporal_grad = lax.optimization_barrier(jnp.sum(results[3], axis=0)) * grad_scale
    return (results[0], results[1], spatial_grad, temporal_grad)
```

```python
import math

import jax
import jax.numpy as jnp
from jax import lax
from jax.experimental import pallas as pl
from jax.experimental.pallas import tpu as pltpu
from jax.sharding import PartitionSpec as P

MESH = pl.DeviceIdType.MESH
ROWS, CH, COLS = 16, 320, 128
PAIRS = ROWS // 2
SHARD = CH // 8
SLAB = 3 * CH
WIDE = 1024
BF16, F32 = jnp.bfloat16, jnp.float32


def remote(src, dst, send_sem, recv_sem, device):
    return pltpu.make_async_remote_copy(
        src_ref=src,
        dst_ref=dst,
        send_sem=send_sem,
        recv_sem=recv_sem,
        device_id=device,
        device_id_type=MESH,
    )


def dot(lhs, rhs):
    return jnp.dot(lhs, rhs, preferred_element_type=F32)


def dot_pixels(lhs, rhs):
    return lax.dot_general(lhs, rhs, (((1,), (1,)), ((), ())), preferred_element_type=F32)


def shifted(value, offset):
    column = lax.broadcasted_iota(jnp.int32, value.shape, 1)
    rolled = pltpu.roll(value, (-offset) % COLS, 1)
    edge = 0 if offset < 0 else COLS - 1
    return jnp.where(column == edge, 0.0, rolled)


def body(
    frames_hbm, spatial_ref, temporal_ref, cot_hbm,
    block_hbm, input_hbm, sgrad_ref, tgrad_ref,
    frames, cot3, act3, pre, xs, pgs, wsrc, wall, wl, wt,
    part, cs, cr, ys, yr, zs, zr, hold, hx, xr, hs, hr, final,
    out_block, out_input,
    load_sem, store_sem,
    cot_send, cot_recv, act_send, act_recv,
    wx_send, wx_recv, wz_send, wz_recv, wy_send, wy_recv, wc_send, wc_recv,
    gc_send, gc_recv, gy_send, gy_recv, gz_send, gz_recv, gx_send, gx_recv,
    gh_send, gh_recv, fz_send, fz_recv, fc_send, fc_recv,
):
    s = lax.axis_index("seq")
    d = lax.axis_index("dp")
    x, ylo = s % 4, s // 4
    core, z, yhi = d % 2, (d // 2) % 4, d // 8
    y = 2 * yhi + ylo

    def device(x_, y_, z_, core_):
        return {"seq": (y_ % 2) * 4 + x_, "dp": (y_ // 2) * 8 + z_ * 2 + core_}

    def along_x(offset):
        return device((x + offset) % 4, y, z, core)

    def along_y(offset):
        return device(x, (y + offset) % 4, z, core)

    def along_z(offset):
        return device(x, y, (z + offset) % 4, core)

    partner = device(x, y, z, 1 - core)
    right = {"seq": jnp.minimum(s + 1, 7), "dp": d}
    left = {"seq": jnp.maximum(s - 1, 0), "dp": d}
    has_right, has_left = s < 7, s > 0
    mine = x // 2 == core

    load_frames = pltpu.make_async_copy(frames_hbm, frames, load_sem.at[0])
    load_cot = pltpu.make_async_copy(cot_hbm, cot3.at[1], load_sem.at[1])
    load_frames.start()
    load_cot.start()

    barrier = pltpu.get_barrier_semaphore()
    for offset in (1, 2, 3):
        for peer in (along_x(offset), along_y(offset), along_z(offset)):
            pl.semaphore_signal(barrier, inc=1, device_id=peer, device_id_type=MESH)
    pl.semaphore_signal(barrier, inc=1, device_id=partner, device_id_type=MESH)

    @pl.when(s == 3)
    def _():
        pl.semaphore_signal(barrier, inc=1, device_id=right, device_id_type=MESH)

    @pl.when(s == 4)
    def _():
        pl.semaphore_signal(barrier, inc=1, device_id=left, device_id_type=MESH)

    for q in range(3):
        wsrc[q] = jnp.concatenate(
            [spatial_ref[3 * a + q].astype(F32) for a in range(3)], axis=1
        ).astype(BF16)
    wsrc[3] = jnp.concatenate(
        [temporal_ref[k].astype(F32) for k in range(3)], axis=1
    ).astype(BF16)

    pl.semaphore_wait(barrier, jnp.where(jnp.logical_or(s == 3, s == 4), 11, 10))

    def weight_x(offset):
        return remote(
            wsrc.at[z], wall.at[z, ylo, x], wx_send.at[offset], wx_recv.at[offset], along_x(offset)
        )

    @pl.when(mine)
    def _():
        wall[z, ylo, x] = wsrc[z]
        for offset in (1, 3, 2):
            weight_x(offset).start()

    def halo(source, slots, pair, to_right, send, recv):
        rows = pl.ds(2 * pair, 2)
        slot, side, target = (0, 0, right) if to_right else (2, 1, left)
        return remote(
            source.at[rows],
            slots.at[slot, rows],
            send.at[side, pair],
            recv.at[side, pair],
            target,
        )

    load_cot.wait()

    def send_cot(pair, carry):
        @pl.when(has_right)
        def _():
            halo(cot3.at[1], cot3, pair, True, cot_send, cot_recv).start()

        @pl.when(has_left)
        def _():
            halo(cot3.at[1], cot3, pair, False, cot_send, cot_recv).start()

        return carry

    lax.fori_loop(0, PAIRS, send_cot, 0)

    load_frames.wait()
    for b in range(3):
        xs[b, pl.ds(0, CH), :] = jnp.zeros((CH, COLS), BF16)
        xs[b, pl.ds(17 * CH, 2 * CH), :] = jnp.zeros((2 * CH, COLS), BF16)
        pgs[b, pl.ds(0, CH), :] = jnp.zeros((CH, COLS), BF16)
        pgs[b, pl.ds(17 * CH, CH), :] = jnp.zeros((CH, COLS), BF16)

    def shift_frames(row, carry):
        value = frames[row]
        wide = value.astype(F32)
        place = pl.ds(pl.multiple_of((row + 1) * CH, 64), CH)
        xs[0, place, :] = shifted(wide, -1).astype(BF16)
        xs[1, place, :] = value
        xs[2, place, :] = shifted(wide, 1).astype(BF16)
        return carry

    lax.fori_loop(0, ROWS, shift_frames, 0)

    @pl.when(s == 0)
    def _():
        cot3[0] = jnp.zeros((ROWS, CH, COLS), BF16)
        act3[0] = jnp.zeros((ROWS, CH, COLS), BF16)

    @pl.when(s == 7)
    def _():
        cot3[2] = jnp.zeros((ROWS, CH, COLS), BF16)
        act3[2] = jnp.zeros((ROWS, CH, COLS), BF16)

    both = pl.ds(2 * core, 2)
    for offset in (1, 3, 2):
        @pl.when((x + 4 - offset) % 4 // 2 == core)
        def _():
            weight_x(offset).wait_recv()

    def weight_z(offset):
        chunk = wall.at[z, ylo, both]
        return remote(chunk, chunk, wz_send.at[offset], wz_recv.at[offset], along_z(offset))

    def weight_y(q, index):
        chunk = wall.at[q, ylo, both]
        target = along_y(jnp.where(q < 2, 1, 3))
        return remote(chunk, chunk, wy_send.at[index], wy_recv.at[index], target)

    def weight_core(q, index):
        chunk = wall.at[q, :, both]
        return remote(chunk, chunk, wc_send.at[index], wc_recv.at[index], partner)

    for offset in (1, 3, 2):
        weight_z(offset).start()
    order = (0, 1, 3, 2)
    for index in order:
        q = (z + 4 - index) % 4
        if index:
            weight_z(index).wait_recv()
        weight_y(q, index).start()
    for index in order:
        weight_y((z + 4 - index) % 4, index).wait_recv()
        weight_core((z + 4 - index) % 4, index).start()
    for index in order:
        weight_core((z + 4 - index) % 4, index).wait_recv()

    def place_weights(q, carry):
        full = jnp.concatenate(
            [wall[q, owner // 4, owner % 4].astype(F32) for owner in range(8)], axis=0
        )
        wl[q] = full.astype(BF16)
        turned = full.T
        wt[q] = jnp.concatenate(
            [turned[CH * a : CH * a + CH] for a in (2, 1, 0)], axis=1
        ).astype(BF16)
        return carry

    lax.fori_loop(0, 4, place_weights, 0)

    def slab_pair(ref, pair):
        first = pl.multiple_of(2 * pair * CH, 128)
        return jnp.concatenate(
            [ref[pl.ds(first, SLAB), :], ref[pl.ds(pl.multiple_of(first + CH, 64), SLAB), :]], axis=1
        )

    def frame_pair(ref, pair):
        return jnp.concatenate(
            [
                jnp.concatenate([ref[k, 2 * pair + i] for k in range(3)], axis=0)
                for i in range(2)
            ],
            axis=1,
        )

    def forward(pair, carry):
        total = dot(wl[0], slab_pair(xs.at[0], pair))
        total += dot(wl[1], slab_pair(xs.at[1], pair))
        total += dot(wl[2], slab_pair(xs.at[2], pair))
        rounded = total.astype(BF16)
        wide = rounded.astype(F32)
        activated = (wide / (1.0 + jnp.exp(-wide))).astype(BF16)
        for i in range(2):
            pre[2 * pair + i] = rounded[:, COLS * i : COLS * i + COLS]
            act3[1, 2 * pair + i] = activated[:, COLS * i : COLS * i + COLS]

        @pl.when(has_right)
        def _():
            halo(act3.at[1], act3, pair, True, act_send, act_recv).start()

        @pl.when(has_left)
        def _():
            halo(act3.at[1], act3, pair, False, act_send, act_recv).start()

        return carry

    lax.fori_loop(0, PAIRS, forward, 0)

    def wait_halo(slots, pair, send, recv):
        @pl.when(has_left)
        def _():
            halo(slots.at[1], slots, pair, True, send, recv).wait_recv()

        @pl.when(has_right)
        def _():
            halo(slots.at[1], slots, pair, False, send, recv).wait_recv()

    def backward(pair, carry):
        wait_halo(cot3, pair, cot_send, cot_recv)
        grad = dot(wt[3], frame_pair(cot3, pair)).astype(BF16)
        for i in range(2):
            row = 2 * pair + i
            act_grad = grad[:, COLS * i : COLS * i + COLS].astype(F32)
            wide = pre[row].astype(F32)
            sig = 1.0 / (1.0 + jnp.exp(-wide))
            value = (act_grad * sig * (1.0 + wide * (1.0 - sig))).astype(BF16)
            wide_value = value.astype(F32)
            place = pl.ds(pl.multiple_of((row + 1) * CH, 64), CH)
            pgs[0, place, :] = shifted(wide_value, 1).astype(BF16)
            pgs[1, place, :] = value
            pgs[2, place, :] = shifted(wide_value, -1).astype(BF16)
        return carry

    lax.fori_loop(0, PAIRS, backward, 0)

    def put(q, start, value, lanes):
        part[q, :, :, pl.ds(start, lanes)] = value.reshape(8, SHARD, lanes)

    def columns(ref, k):
        return [
            jnp.concatenate([ref[k, 2 * j], ref[k, 2 * j + 1]], axis=1) for j in range(PAIRS)
        ]

    def temporal_part(k, carry):
        low = jnp.zeros((CH, 256), F32)
        high = jnp.zeros((CH, 128), F32)
        for j in range(PAIRS):
            lhs = jnp.concatenate([cot3[k, 2 * j], cot3[k, 2 * j + 1]], axis=1)
            rhs = jnp.concatenate([act3[1, 2 * j], act3[1, 2 * j + 1]], axis=1)
            low += dot_pixels(lhs, rhs[:256])
            high += dot_pixels(lhs, rhs[192:])
        part[3, :, :, pl.ds(pl.multiple_of(256 * k, 128), 256)] = low.reshape(8, SHARD, 256)
        hold[k] = high
        return carry

    lax.fori_loop(0, 3, temporal_part, 0)
    lane = lax.broadcasted_iota(jnp.int32, (CH, 128), 1)
    put(3, 768, jnp.where(lane < 64, pltpu.roll(hold[0], 64, 1), hold[1]), 128)
    put(3, 896, pltpu.roll(hold[2], 64, 1), 128)

    def spatial_part(b):
        def block(n, carry):
            total = jnp.zeros((CH, 256), F32)
            for j in range(PAIRS):
                lhs = jnp.concatenate(
                    [
                        pgs[b, pl.ds((2 * j + 1) * CH, CH), :],
                        pgs[b, pl.ds((2 * j + 2) * CH, CH), :],
                    ],
                    axis=1,
                )
                base = pl.multiple_of(n * 256, 256)
                rhs = jnp.concatenate(
                    [
                        xs[1, pl.ds(base + 2 * j * CH, 256), :],
                        xs[1, pl.ds(base + (2 * j + 1) * CH, 256), :],
                    ],
                    axis=1,
                )
                total += dot_pixels(lhs, rhs)
            part[b, :, :, pl.ds(pl.multiple_of(n * 256, 256), 256)] = total.reshape(8, SHARD, 256)
            return carry

        lax.fori_loop(0, 4, block, 0)

    def owned(q, half, pair_core):
        return part[q, pl.ds(4 * half + 2 * pair_core, 2)]

    def grad_core(q):
        return remote(cs.at[q], cr.at[q], gc_send.at[q], gc_recv.at[q], partner)

    def grad_y(q):
        return remote(ys.at[q], yr.at[q], gy_send.at[q], gy_recv.at[q], along_y(1 if q < 2 else 3))

    def grad_z(q):
        offset = (q + 4 - z) % 4
        return remote(
            zs.at[q], zr.at[offset], gz_send.at[offset], gz_recv.at[offset],
            device(x, y, q, core),
        )

    def start_core(q):
        for half in range(2):
            cs[q, half] = owned(q, half, 1 - core).astype(BF16)
        grad_core(q).start()

    def core_to_y(q):
        grad_core(q).wait_recv()
        for half in range(2):
            place = pl.ds(4 * half + 2 * core, 2)
            part[q, place] = part[q, place] + cr[q, half].astype(F32)
        ys[q] = owned(q, 1 - ylo, core).astype(BF16)
        grad_y(q).start()

    def y_to_z(q):
        grad_y(q).wait_recv()
        place = pl.ds(4 * ylo + 2 * core, 2)
        part[q, place] = part[q, place] + yr[q].astype(F32)

        @pl.when(z != q)
        def _():
            zs[q] = part[q, place].astype(BF16)
            grad_z(q).start()

    def wait_z(offset):
        remote(
            zs.at[0], zr.at[offset], gz_send.at[offset], gz_recv.at[offset], along_z(offset)
        ).wait_recv()

    def grad_x(i):
        owner = 2 * core + i
        offset = (owner + 4 - x) % 4
        return remote(
            hx.at[i], xr.at[offset], gx_send.at[offset], gx_recv.at[offset],
            device(owner, y, z, core),
        )

    def z_to_x():
        total = part[z, pl.ds(4 * ylo + 2 * core, 2)]
        for offset in (1, 2, 3):
            wait_z(offset)
            total = total + zr[offset].astype(F32)
        part[z, pl.ds(4 * ylo + 2 * core, 2)] = total
        hx[...] = total.astype(BF16)
        for i in range(2):
            @pl.when(2 * core + i != x)
            def _():
                grad_x(i).start()

    grad_h = remote(hs, hr, gh_send.at[0], gh_recv.at[0], along_y(2))

    def x_to_h():
        @pl.when(mine)
        def _():
            total = part[z, s]
            for offset in (1, 2, 3):
                remote(
                    hx.at[0], xr.at[offset], gx_send.at[offset], gx_recv.at[offset],
                    along_x(offset),
                ).wait_recv()
                total = total + xr[offset].astype(F32)
            hs[...] = total.astype(BF16)
            grad_h.start()

    def final_z(offset):
        return remote(
            final.at[z], final.at[z], fz_send.at[offset], fz_recv.at[offset], along_z(offset)
        )

    def h_to_final():
        @pl.when(mine)
        def _():
            grad_h.wait_recv()
            final[z] = hs[...].astype(F32) + hr[...].astype(F32)
            for offset in (1, 3, 2):
                final_z(offset).start()

    final_core = remote(final, final, fc_send.at[0], fc_recv.at[0], partner)

    def final_to_core():
        @pl.when(mine)
        def _():
            for offset in (1, 3, 2):
                final_z(offset).wait_recv()
            final_core.start()

    start_core(3)
    spatial_part(0)
    start_core(0)
    core_to_y(3)
    spatial_part(1)
    start_core(1)
    core_to_y(0)
    y_to_z(3)
    spatial_part(2)
    start_core(2)
    core_to_y(1)
    y_to_z(0)

    def store_rows(source, target, pair, which):
        rows = pl.ds(2 * pair, 2)
        return pltpu.make_async_copy(source.at[rows], target.at[rows], store_sem.at[which, pair])

    def input_grad(pair, carry):
        total = dot(wt[0], slab_pair(pgs.at[0], pair))
        total += dot(wt[1], slab_pair(pgs.at[1], pair))
        total += dot(wt[2], slab_pair(pgs.at[2], pair))
        for i in range(2):
            row = 2 * pair + i
            value = cot3[1, row].astype(F32) + total[:, COLS * i : COLS * i + COLS]
            out_input[row] = value.astype(BF16)
        store_rows(out_input, input_hbm, pair, 0).start()

        @pl.when(pair == 1)
        def _():
            core_to_y(2)
            y_to_z(1)

        @pl.when(pair == 5)
        def _():
            y_to_z(2)

        return carry

    lax.fori_loop(0, PAIRS, input_grad, 0)

    z_to_x()

    def temporal(pair, carry):
        wait_halo(act3, pair, act_send, act_recv)
        value = dot(wl[3], frame_pair(act3, pair)).astype(BF16).astype(F32)
        for i in range(2):
            row = 2 * pair + i
            total = frames[row].astype(F32) + value[:, COLS * i : COLS * i + COLS]
            out_block[row] = total.astype(BF16)
        store_rows(out_block, block_hbm, pair, 1).start()

        @pl.when(pair == 2)
        def _():
            x_to_h()

        @pl.when(pair == 4)
        def _():
            h_to_final()

        @pl.when(pair == 6)
        def _():
            final_to_core()

        return carry

    lax.fori_loop(0, PAIRS, temporal, 0)

    @pl.when(jnp.logical_not(mine))
    def _():
        final_core.wait_recv()

    scale = 1.0 / math.sqrt(16 * 8 * ROWS * COLS)
    for b in range(3):
        value = final[b] * scale
        for a in range(3):
            sgrad_ref[3 * a + b] = value[:, CH * a : CH * a + CH]
    value = final[3] * scale
    for slot in range(3):
        tgrad_ref[2 - slot] = jnp.concatenate(
            [
                value[:, 256 * slot : 256 * slot + 256],
                value[:, 768 + 64 * slot : 768 + 64 * slot + 64],
            ],
            axis=1,
        )

    def drain(pair, carry):
        @pl.when(has_right)
        def _():
            halo(cot3.at[1], cot3, pair, True, cot_send, cot_recv).wait_send()
            halo(act3.at[1], act3, pair, True, act_send, act_recv).wait_send()

        @pl.when(has_left)
        def _():
            halo(cot3.at[1], cot3, pair, False, cot_send, cot_recv).wait_send()
            halo(act3.at[1], act3, pair, False, act_send, act_recv).wait_send()

        store_rows(out_input, input_hbm, pair, 0).wait()
        store_rows(out_block, block_hbm, pair, 1).wait()
        return carry

    lax.fori_loop(0, PAIRS, drain, 0)

    @pl.when(mine)
    def _():
        for offset in (1, 2, 3):
            weight_x(offset).wait_send()
            final_z(offset).wait_send()
        grad_h.wait_send()
        final_core.wait_send()

    for offset in (1, 2, 3):
        weight_z(offset).wait_send()
    for index in range(4):
        q = (z + 4 - index) % 4
        weight_y(q, index).wait_send()
        weight_core(q, index).wait_send()
        grad_core(index).wait_send()
        grad_y(index).wait_send()

        @pl.when(z != index)
        def _():
            grad_z(index).wait_send()

    for i in range(2):
        @pl.when(2 * core + i != x)
        def _():
            grad_x(i).wait_send()


def local(frames_in, spatial_kernel, temporal_kernel, out_cotangent):
    image = (ROWS, CH, COLS)
    dma = pltpu.SemaphoreType.DMA
    anywhere = pl.BlockSpec(memory_space=pl.ANY)
    vmem = pl.BlockSpec(memory_space=pltpu.VMEM)
    chunk = (SHARD, WIDE)
    block_out, input_grad, spatial_grad, temporal_grad = pl.pallas_call(
        body,
        out_shape=(
            jax.ShapeDtypeStruct(image, BF16),
            jax.ShapeDtypeStruct(image, BF16),
            jax.ShapeDtypeStruct((9, SHARD, CH), F32),
            jax.ShapeDtypeStruct((3, SHARD, CH), F32),
        ),
        in_specs=[anywhere, vmem, vmem, anywhere],
        out_specs=[anywhere, anywhere, vmem, vmem],
        scratch_shapes=[
            pltpu.VMEM(image, BF16),
            pltpu.VMEM((3,) + image, BF16),
            pltpu.VMEM((3,) + image, BF16),
            pltpu.VMEM(image, BF16),
            pltpu.VMEM((3, 19 * CH, COLS), BF16),
            pltpu.VMEM((3, 18 * CH, COLS), BF16),
            pltpu.VMEM((4, SHARD, SLAB), BF16),
            pltpu.VMEM((4, 2, 4, SHARD, SLAB), BF16),
            pltpu.VMEM((4, CH, SLAB), BF16),
            pltpu.VMEM((4, CH, SLAB), BF16),
            pltpu.VMEM((4, 8) + chunk, F32),
            pltpu.VMEM((4, 2, 2) + chunk, BF16),
            pltpu.VMEM((4, 2, 2) + chunk, BF16),
            pltpu.VMEM((4, 2) + chunk, BF16),
            pltpu.VMEM((4, 2) + chunk, BF16),
            pltpu.VMEM((4, 2) + chunk, BF16),
            pltpu.VMEM((4, 2) + chunk, BF16),
            pltpu.VMEM((3, CH, 128), F32),
            pltpu.VMEM((2,) + chunk, BF16),
            pltpu.VMEM((4,) + chunk, BF16),
            pltpu.VMEM(chunk, BF16),
            pltpu.VMEM(chunk, BF16),
            pltpu.VMEM((4,) + chunk, F32),
            pltpu.VMEM(image, BF16),
            pltpu.VMEM(image, BF16),
            dma((2,)),
            dma((2, PAIRS)),
            dma((2, PAIRS)), dma((2, PAIRS)), dma((2, PAIRS)), dma((2, PAIRS)),
            dma((4,)), dma((4,)), dma((4,)), dma((4,)),
            dma((4,)), dma((4,)), dma((4,)), dma((4,)),
            dma((4,)), dma((4,)), dma((4,)), dma((4,)),
            dma((4,)), dma((4,)), dma((4,)), dma((4,)),
            dma((1,)), dma((1,)), dma((4,)), dma((4,)), dma((1,)), dma((1,)),
        ],
        compiler_params=pltpu.CompilerParams(
            collective_id=0, has_side_effects=True, vmem_limit_bytes=67043328
        ),
        name="block",
    )(frames_in[0, 0], spatial_kernel, temporal_kernel, out_cotangent[0, 0])
    return block_out[None, None], input_grad[None, None], spatial_grad, temporal_grad


def solution(mesh):
    placed = (
        P("dp", "seq", None, None, None),
        P(None, "seq", None),
        P(None, "seq", None),
        P("dp", "seq", None, None, None),
    )
    return jax.shard_map(
        local,
        mesh=mesh,
        in_specs=placed,
        out_specs=(
            P("dp", "seq", None, None, None),
            P("dp", "seq", None, None, None),
            P(None, "seq", None),
            P(None, "seq", None),
        ),
        check_vma=False,
    )
```

```python
import math

import jax
import jax.numpy as jnp
from jax import lax
from jax.experimental import pallas as pl
from jax.experimental.pallas import tpu as pltpu
from jax.sharding import PartitionSpec as P

MESH = pl.DeviceIdType.MESH
ROWS, CH, COLS = 16, 320, 128
PAIRS = ROWS // 2
SHARD = CH // 8
SLAB = 3 * CH
WIDE = 1024
FINAL = ((1, 0), (3, 0), (1, 1), (3, 1), (2, 0), (2, 1), (0, 1))
BF16, F32 = jnp.bfloat16, jnp.float32


def remote(src, dst, send_sem, recv_sem, device):
    return pltpu.make_async_remote_copy(
        src_ref=src,
        dst_ref=dst,
        send_sem=send_sem,
        recv_sem=recv_sem,
        device_id=device,
        device_id_type=MESH,
    )


def dot(lhs, rhs):
    return jnp.dot(lhs, rhs, preferred_element_type=F32)


def dot_pixels(lhs, rhs):
    return lax.dot_general(lhs, rhs, (((1,), (1,)), ((), ())), preferred_element_type=F32)


def shifted(value, offset):
    column = lax.broadcasted_iota(jnp.int32, value.shape, 1)
    rolled = pltpu.roll(value, (-offset) % COLS, 1)
    edge = 0 if offset < 0 else COLS - 1
    return jnp.where(column == edge, 0.0, rolled)


def body(
    frames_hbm, spatial_ref, temporal_ref, cot_hbm,
    block_hbm, input_hbm, sgrad_ref, tgrad_ref,
    frames, cot3, act3, pre, xs, pgs, wsrc, wall, wl, wt,
    part, cs, cr, ys, yr, zs, zr, hold, hx, xr, hs, hr, final,
    out_block, out_input,
    load_sem, store_sem,
    cot_send, cot_recv, act_send, act_recv,
    wx_send, wx_recv, wz_send, wz_recv, wy_send, wy_recv, wc_send, wc_recv,
    gc_send, gc_recv, gy_send, gy_recv, gz_send, gz_recv, gx_send, gx_recv,
    gh_send, gh_recv, fz_send, fz_recv,
):
    s = lax.axis_index("seq")
    d = lax.axis_index("dp")
    x, ylo = s % 4, s // 4
    core, z, yhi = d % 2, (d // 2) % 4, d // 8
    y = 2 * yhi + ylo

    def device(x_, y_, z_, core_):
        return {"seq": (y_ % 2) * 4 + x_, "dp": (y_ // 2) * 8 + z_ * 2 + core_}

    def along_x(offset):
        return device((x + offset) % 4, y, z, core)

    def along_y(offset):
        return device(x, (y + offset) % 4, z, core)

    def along_z(offset):
        return device(x, y, (z + offset) % 4, core)

    partner = device(x, y, z, 1 - core)
    right = {"seq": jnp.minimum(s + 1, 7), "dp": d}
    left = {"seq": jnp.maximum(s - 1, 0), "dp": d}
    has_right, has_left = s < 7, s > 0
    busy, quiet = jnp.where(ylo == 0, 1, 3), jnp.where(ylo == 0, 3, 1)
    mine = x // 2 == core

    load_frames = pltpu.make_async_copy(frames_hbm, frames, load_sem.at[0])
    load_cot = pltpu.make_async_copy(cot_hbm, cot3.at[1], load_sem.at[1])
    load_frames.start()
    load_cot.start()

    barrier = pltpu.get_barrier_semaphore()
    for offset in (1, 2, 3):
        for peer in (along_x(offset), along_y(offset), along_z(offset)):
            pl.semaphore_signal(barrier, inc=1, device_id=peer, device_id_type=MESH)
    pl.semaphore_signal(barrier, inc=1, device_id=partner, device_id_type=MESH)
    for offset in (1, 2, 3):
        crossed = device(x, y, (z + offset) % 4, 1 - core)
        pl.semaphore_signal(barrier, inc=1, device_id=crossed, device_id_type=MESH)

    @pl.when(s == 3)
    def _():
        pl.semaphore_signal(barrier, inc=1, device_id=right, device_id_type=MESH)

    @pl.when(s == 4)
    def _():
        pl.semaphore_signal(barrier, inc=1, device_id=left, device_id_type=MESH)

    for q in range(3):
        wsrc[q] = jnp.concatenate(
            [spatial_ref[3 * a + q].astype(F32) for a in range(3)], axis=1
        ).astype(BF16)
    wsrc[3] = jnp.concatenate(
        [temporal_ref[k].astype(F32) for k in range(3)], axis=1
    ).astype(BF16)

    pl.semaphore_wait(barrier, jnp.where(jnp.logical_or(s == 3, s == 4), 14, 13))

    def weight_x(offset):
        return remote(
            wsrc.at[z], wall.at[z, ylo, x], wx_send.at[offset], wx_recv.at[offset], along_x(offset)
        )

    @pl.when(mine)
    def _():
        wall[z, ylo, x] = wsrc[z]
        for offset in (1, 3, 2):
            weight_x(offset).start()

    def halo(source, slots, pair, to_right, send, recv):
        rows = pl.ds(2 * pair, 2)
        slot, side, target = (0, 0, right) if to_right else (2, 1, left)
        return remote(
            source.at[rows],
            slots.at[slot, rows],
            send.at[side, pair],
            recv.at[side, pair],
            target,
        )

    both = pl.ds(2 * core, 2)
    for offset in (1, 3, 2):
        @pl.when((x + 4 - offset) % 4 // 2 == core)
        def _():
            weight_x(offset).wait_recv()

    def weight_z(offset):
        chunk = wall.at[z, ylo, both]
        return remote(chunk, chunk, wz_send.at[offset], wz_recv.at[offset], along_z(offset))

    def weight_y(q, index):
        chunk = wall.at[q, ylo, both]
        target = along_y(quiet if index else busy)
        return remote(chunk, chunk, wy_send.at[index], wy_recv.at[index], target)

    def weight_core(q, index):
        chunk = wall.at[q, :, both]
        return remote(chunk, chunk, wc_send.at[index], wc_recv.at[index], partner)

    for offset in (1, 3, 2):
        weight_z(offset).start()
    weight_y(z, 0).start()

    load_cot.wait()

    def send_cot(pair, carry):
        @pl.when(has_right)
        def _():
            halo(cot3.at[1], cot3, pair, True, cot_send, cot_recv).start()

        @pl.when(has_left)
        def _():
            halo(cot3.at[1], cot3, pair, False, cot_send, cot_recv).start()

        return carry

    lax.fori_loop(0, PAIRS, send_cot, 0)

    load_frames.wait()
    for b in range(3):
        xs[b, pl.ds(0, CH), :] = jnp.zeros((CH, COLS), BF16)
        xs[b, pl.ds(17 * CH, 2 * CH), :] = jnp.zeros((2 * CH, COLS), BF16)
        pgs[b, pl.ds(0, CH), :] = jnp.zeros((CH, COLS), BF16)
        pgs[b, pl.ds(17 * CH, CH), :] = jnp.zeros((CH, COLS), BF16)

    def shift_frames(row, carry):
        value = frames[row]
        wide = value.astype(F32)
        place = pl.ds(pl.multiple_of((row + 1) * CH, 64), CH)
        xs[0, place, :] = shifted(wide, -1).astype(BF16)
        xs[1, place, :] = value
        xs[2, place, :] = shifted(wide, 1).astype(BF16)
        return carry

    lax.fori_loop(0, ROWS, shift_frames, 0)

    @pl.when(s == 0)
    def _():
        cot3[0] = jnp.zeros((ROWS, CH, COLS), BF16)
        act3[0] = jnp.zeros((ROWS, CH, COLS), BF16)

    @pl.when(s == 7)
    def _():
        cot3[2] = jnp.zeros((ROWS, CH, COLS), BF16)
        act3[2] = jnp.zeros((ROWS, CH, COLS), BF16)

    order = (0, 1, 3, 2)
    for index in order:
        if index:
            weight_z(index).wait_recv()
            weight_y((z + 4 - index) % 4, index).start()
    for index in order:
        weight_y((z + 4 - index) % 4, index).wait_recv()
        weight_core((z + 4 - index) % 4, index).start()
    for index in order:
        weight_core((z + 4 - index) % 4, index).wait_recv()

    def place_weights(q, carry):
        full = jnp.concatenate(
            [wall[q, owner // 4, owner % 4].astype(F32) for owner in range(8)], axis=0
        )
        wl[q] = full.astype(BF16)
        return carry

    lax.fori_loop(0, 4, place_weights, 0)

    def turn_weights(q, carry):
        turned = wl[q].astype(F32).T
        wt[q] = jnp.concatenate(
            [turned[CH * a : CH * a + CH] for a in (2, 1, 0)], axis=1
        ).astype(BF16)
        return carry

    def slab_pair(ref, pair):
        first = pl.multiple_of(2 * pair * CH, 128)
        return jnp.concatenate(
            [ref[pl.ds(first, SLAB), :], ref[pl.ds(pl.multiple_of(first + CH, 64), SLAB), :]], axis=1
        )

    def frame_pair(ref, pair):
        return jnp.concatenate(
            [
                jnp.concatenate([ref[k, 2 * pair + i] for k in range(3)], axis=0)
                for i in range(2)
            ],
            axis=1,
        )

    def forward(pair, carry):
        total = dot(wl[0], slab_pair(xs.at[0], pair))
        total += dot(wl[1], slab_pair(xs.at[1], pair))
        total += dot(wl[2], slab_pair(xs.at[2], pair))
        rounded = total.astype(BF16)
        wide = rounded.astype(F32)
        activated = (wide / (1.0 + jnp.exp(-wide))).astype(BF16)
        for i in range(2):
            pre[2 * pair + i] = rounded[:, COLS * i : COLS * i + COLS]
            act3[1, 2 * pair + i] = activated[:, COLS * i : COLS * i + COLS]

        @pl.when(has_right)
        def _():
            halo(act3.at[1], act3, pair, True, act_send, act_recv).start()

        @pl.when(has_left)
        def _():
            halo(act3.at[1], act3, pair, False, act_send, act_recv).start()

        return carry

    lax.fori_loop(0, PAIRS, forward, 0)
    lax.fori_loop(0, 4, turn_weights, 0)

    def wait_halo(slots, pair, send, recv):
        @pl.when(has_left)
        def _():
            halo(slots.at[1], slots, pair, True, send, recv).wait_recv()

        @pl.when(has_right)
        def _():
            halo(slots.at[1], slots, pair, False, send, recv).wait_recv()

    def backward(pair, carry):
        wait_halo(cot3, pair, cot_send, cot_recv)
        grad = dot(wt[3], frame_pair(cot3, pair)).astype(BF16)
        for i in range(2):
            row = 2 * pair + i
            act_grad = grad[:, COLS * i : COLS * i + COLS].astype(F32)
            wide = pre[row].astype(F32)
            sig = 1.0 / (1.0 + jnp.exp(-wide))
            value = (act_grad * sig * (1.0 + wide * (1.0 - sig))).astype(BF16)
            wide_value = value.astype(F32)
            place = pl.ds(pl.multiple_of((row + 1) * CH, 64), CH)
            pgs[0, place, :] = shifted(wide_value, 1).astype(BF16)
            pgs[1, place, :] = value
            pgs[2, place, :] = shifted(wide_value, -1).astype(BF16)
        return carry

    lax.fori_loop(0, PAIRS, backward, 0)

    def put(q, start, value, lanes):
        part[q, :, :, pl.ds(start, lanes)] = value.reshape(8, SHARD, lanes)

    def columns(ref, k):
        return [
            jnp.concatenate([ref[k, 2 * j], ref[k, 2 * j + 1]], axis=1) for j in range(PAIRS)
        ]

    def temporal_part(k, carry):
        low = jnp.zeros((CH, 256), F32)
        high = jnp.zeros((CH, 128), F32)
        for j in range(PAIRS):
            lhs = jnp.concatenate([cot3[k, 2 * j], cot3[k, 2 * j + 1]], axis=1)
            rhs = jnp.concatenate([act3[1, 2 * j], act3[1, 2 * j + 1]], axis=1)
            low += dot_pixels(lhs, rhs[:256])
            high += dot_pixels(lhs, rhs[192:])
        part[3, :, :, pl.ds(pl.multiple_of(256 * k, 128), 256)] = low.reshape(8, SHARD, 256)
        hold[k] = high
        return carry

    lax.fori_loop(0, 3, temporal_part, 0)
    lane = lax.broadcasted_iota(jnp.int32, (CH, 128), 1)
    put(3, 768, jnp.where(lane < 64, pltpu.roll(hold[0], 64, 1), hold[1]), 128)
    put(3, 896, pltpu.roll(hold[2], 64, 1), 128)

    def spatial_part(b):
        def block(n, carry):
            total = jnp.zeros((CH, 256), F32)
            for j in range(PAIRS):
                lhs = jnp.concatenate(
                    [
                        pgs[b, pl.ds((2 * j + 1) * CH, CH), :],
                        pgs[b, pl.ds((2 * j + 2) * CH, CH), :],
                    ],
                    axis=1,
                )
                base = pl.multiple_of(n * 256, 256)
                rhs = jnp.concatenate(
                    [
                        xs[1, pl.ds(base + 2 * j * CH, 256), :],
                        xs[1, pl.ds(base + (2 * j + 1) * CH, 256), :],
                    ],
                    axis=1,
                )
                total += dot_pixels(lhs, rhs)
            part[b, :, :, pl.ds(pl.multiple_of(n * 256, 256), 256)] = total.reshape(8, SHARD, 256)
            return carry

        lax.fori_loop(0, 4, block, 0)

    def owned(q, half, pair_core):
        return part[q, pl.ds(4 * half + 2 * pair_core, 2)]

    def grad_core(q):
        return remote(cs.at[q], cr.at[q], gc_send.at[q], gc_recv.at[q], partner)

    def grad_y(q):
        return remote(ys.at[q], yr.at[q], gy_send.at[q], gy_recv.at[q], along_y(quiet))

    def grad_z(q):
        offset = (q + 4 - z) % 4
        return remote(
            zs.at[q], zr.at[offset], gz_send.at[offset], gz_recv.at[offset],
            device(x, y, q, core),
        )

    def start_core(q):
        for half in range(2):
            cs[q, half] = owned(q, half, 1 - core).astype(BF16)
        grad_core(q).start()

    def core_to_y(q):
        grad_core(q).wait_recv()
        for half in range(2):
            place = pl.ds(4 * half + 2 * core, 2)
            part[q, place] = part[q, place] + cr[q, half].astype(F32)
        ys[q] = owned(q, 1 - ylo, core).astype(BF16)
        grad_y(q).start()

    def y_to_z(q):
        grad_y(q).wait_recv()
        place = pl.ds(4 * ylo + 2 * core, 2)
        part[q, place] = part[q, place] + yr[q].astype(F32)

        @pl.when(z != q)
        def _():
            zs[q] = part[q, place].astype(BF16)
            grad_z(q).start()

    def wait_z(offset):
        remote(
            zs.at[0], zr.at[offset], gz_send.at[offset], gz_recv.at[offset], along_z(offset)
        ).wait_recv()

    def grad_x(i):
        owner = 2 * core + i
        offset = (owner + 4 - x) % 4
        return remote(
            hx.at[i], xr.at[offset], gx_send.at[offset], gx_recv.at[offset],
            device(owner, y, z, core),
        )

    def z_to_x():
        total = part[z, pl.ds(4 * ylo + 2 * core, 2)]
        for offset in (1, 2, 3):
            wait_z(offset)
            total = total + zr[offset].astype(F32)
        part[z, pl.ds(4 * ylo + 2 * core, 2)] = total
        hx[...] = total.astype(BF16)
        for i in range(2):
            @pl.when(2 * core + i != x)
            def _():
                grad_x(i).start()

    grad_h = remote(hs, hr, gh_send.at[0], gh_recv.at[0], along_y(2))

    def x_to_h():
        @pl.when(mine)
        def _():
            total = part[z, s]
            for offset in (1, 2, 3):
                remote(
                    hx.at[0], xr.at[offset], gx_send.at[offset], gx_recv.at[offset],
                    along_x(offset),
                ).wait_recv()
                total = total + xr[offset].astype(F32)
            hs[...] = total.astype(BF16)
            grad_h.start()

    def final_send(offset, cross):
        target = device(x, y, (z + offset) % 4, core + cross - 2 * core * cross)
        return remote(
            final.at[z], final.at[z], fz_send.at[offset, cross], fz_recv.at[offset], target
        )

    def h_to_final():
        @pl.when(mine)
        def _():
            grad_h.wait_recv()
            final[z] = (hs[...].astype(F32) + hr[...].astype(F32)).astype(BF16)
            for offset, cross in FINAL:
                final_send(offset, cross).start()

    start_core(3)
    spatial_part(0)
    start_core(0)
    core_to_y(3)
    spatial_part(1)
    start_core(1)
    core_to_y(0)
    y_to_z(3)
    spatial_part(2)
    start_core(2)
    core_to_y(1)
    y_to_z(0)

    def store_rows(source, target, pair, which):
        rows = pl.ds(2 * pair, 2)
        return pltpu.make_async_copy(source.at[rows], target.at[rows], store_sem.at[which, pair])

    def input_grad(pair, carry):
        total = dot(wt[0], slab_pair(pgs.at[0], pair))
        total += dot(wt[1], slab_pair(pgs.at[1], pair))
        total += dot(wt[2], slab_pair(pgs.at[2], pair))
        for i in range(2):
            row = 2 * pair + i
            value = cot3[1, row].astype(F32) + total[:, COLS * i : COLS * i + COLS]
            out_input[row] = value.astype(BF16)
        store_rows(out_input, input_hbm, pair, 0).start()

        @pl.when(pair == 1)
        def _():
            core_to_y(2)
            y_to_z(1)

        @pl.when(pair == 5)
        def _():
            y_to_z(2)

        return carry

    lax.fori_loop(0, PAIRS, input_grad, 0)

    z_to_x()

    def temporal(pair, carry):
        wait_halo(act3, pair, act_send, act_recv)
        value = dot(wl[3], frame_pair(act3, pair)).astype(BF16).astype(F32)
        for i in range(2):
            row = 2 * pair + i
            total = frames[row].astype(F32) + value[:, COLS * i : COLS * i + COLS]
            out_block[row] = total.astype(BF16)
        store_rows(out_block, block_hbm, pair, 1).start()

        @pl.when(pair == 2)
        def _():
            x_to_h()

        @pl.when(pair == 4)
        def _():
            h_to_final()

        return carry

    lax.fori_loop(0, PAIRS, temporal, 0)

    for offset in (1, 3, 2):
        final_send(offset, 0).wait_recv()

    @pl.when(jnp.logical_not(mine))
    def _():
        final_send(0, 1).wait_recv()

    scale = 1.0 / math.sqrt(16 * 8 * ROWS * COLS)
    for b in range(3):
        value = final[b].astype(F32) * scale
        for a in range(3):
            sgrad_ref[3 * a + b] = value[:, CH * a : CH * a + CH]
    value = final[3].astype(F32) * scale
    for slot in range(3):
        tgrad_ref[2 - slot] = jnp.concatenate(
            [
                value[:, 256 * slot : 256 * slot + 256],
                value[:, 768 + 64 * slot : 768 + 64 * slot + 64],
            ],
            axis=1,
        )

    def drain(pair, carry):
        @pl.when(has_right)
        def _():
            halo(cot3.at[1], cot3, pair, True, cot_send, cot_recv).wait_send()
            halo(act3.at[1], act3, pair, True, act_send, act_recv).wait_send()

        @pl.when(has_left)
        def _():
            halo(cot3.at[1], cot3, pair, False, cot_send, cot_recv).wait_send()
            halo(act3.at[1], act3, pair, False, act_send, act_recv).wait_send()

        store_rows(out_input, input_hbm, pair, 0).wait()
        store_rows(out_block, block_hbm, pair, 1).wait()
        return carry

    lax.fori_loop(0, PAIRS, drain, 0)

    @pl.when(mine)
    def _():
        for offset in (1, 2, 3):
            weight_x(offset).wait_send()
        for offset, cross in FINAL:
            final_send(offset, cross).wait_send()
        grad_h.wait_send()

    for offset in (1, 2, 3):
        weight_z(offset).wait_send()
    for index in range(4):
        q = (z + 4 - index) % 4
        weight_y(q, index).wait_send()
        weight_core(q, index).wait_send()
        grad_core(index).wait_send()
        grad_y(index).wait_send()

        @pl.when(z != index)
        def _():
            grad_z(index).wait_send()

    for i in range(2):
        @pl.when(2 * core + i != x)
        def _():
            grad_x(i).wait_send()


def local(frames_in, spatial_kernel, temporal_kernel, out_cotangent):
    image = (ROWS, CH, COLS)
    dma = pltpu.SemaphoreType.DMA
    anywhere = pl.BlockSpec(memory_space=pl.ANY)
    vmem = pl.BlockSpec(memory_space=pltpu.VMEM)
    chunk = (SHARD, WIDE)
    block_out, input_grad, spatial_grad, temporal_grad = pl.pallas_call(
        body,
        out_shape=(
            jax.ShapeDtypeStruct(image, BF16),
            jax.ShapeDtypeStruct(image, BF16),
            jax.ShapeDtypeStruct((9, SHARD, CH), F32),
            jax.ShapeDtypeStruct((3, SHARD, CH), F32),
        ),
        in_specs=[anywhere, vmem, vmem, anywhere],
        out_specs=[anywhere, anywhere, vmem, vmem],
        scratch_shapes=[
            pltpu.VMEM(image, BF16),
            pltpu.VMEM((3,) + image, BF16),
            pltpu.VMEM((3,) + image, BF16),
            pltpu.VMEM(image, BF16),
            pltpu.VMEM((3, 19 * CH, COLS), BF16),
            pltpu.VMEM((3, 18 * CH, COLS), BF16),
            pltpu.VMEM((4, SHARD, SLAB), BF16),
            pltpu.VMEM((4, 2, 4, SHARD, SLAB), BF16),
            pltpu.VMEM((4, CH, SLAB), BF16),
            pltpu.VMEM((4, CH, SLAB), BF16),
            pltpu.VMEM((4, 8) + chunk, F32),
            pltpu.VMEM((4, 2, 2) + chunk, BF16),
            pltpu.VMEM((4, 2, 2) + chunk, BF16),
            pltpu.VMEM((4, 2) + chunk, BF16),
            pltpu.VMEM((4, 2) + chunk, BF16),
            pltpu.VMEM((4, 2) + chunk, BF16),
            pltpu.VMEM((4, 2) + chunk, BF16),
            pltpu.VMEM((3, CH, 128), F32),
            pltpu.VMEM((2,) + chunk, BF16),
            pltpu.VMEM((4,) + chunk, BF16),
            pltpu.VMEM(chunk, BF16),
            pltpu.VMEM(chunk, BF16),
            pltpu.VMEM((4,) + chunk, BF16),
            pltpu.VMEM(image, BF16),
            pltpu.VMEM(image, BF16),
            dma((2,)),
            dma((2, PAIRS)),
            dma((2, PAIRS)), dma((2, PAIRS)), dma((2, PAIRS)), dma((2, PAIRS)),
            dma((4,)), dma((4,)), dma((4,)), dma((4,)),
            dma((4,)), dma((4,)), dma((4,)), dma((4,)),
            dma((4,)), dma((4,)), dma((4,)), dma((4,)),
            dma((4,)), dma((4,)), dma((4,)), dma((4,)),
            dma((1,)), dma((1,)), dma((4, 2)), dma((4,)),
        ],
        compiler_params=pltpu.CompilerParams(
            collective_id=0, has_side_effects=True, vmem_limit_bytes=67043328
        ),
        name="block",
    )(frames_in[0, 0], spatial_kernel, temporal_kernel, out_cotangent[0, 0])
    return block_out[None, None], input_grad[None, None], spatial_grad, temporal_grad


def solution(mesh):
    placed = (
        P("dp", "seq", None, None, None),
        P(None, "seq", None),
        P(None, "seq", None),
        P("dp", "seq", None, None, None),
    )
    return jax.shard_map(
        local,
        mesh=mesh,
        in_specs=placed,
        out_specs=(
            P("dp", "seq", None, None, None),
            P("dp", "seq", None, None, None),
            P(None, "seq", None),
            P(None, "seq", None),
        ),
        check_vma=False,
    )
```
